32 devices in a mesh: lat: 4 (over y, x), lon: 4 (over z), var: 2 (over core).
Axes of the slice: x: 2, y: 2, z: 4, core: 2. Of those that a mesh axis runs over, the one named last changes fastest.
Arguments:
- control: float32 [6, 4, 128, 512], P('var', None, 'lat', 'lon'), may hold values from -6 to 6
- gradient: float32 [6, 4, 128, 512], P('var', None, 'lat', 'lon'), may hold values from -6 to 6
- std_dev: float32 [6, 128, 512], P('var', 'lat', 'lon'), may hold values from 0.3 to 3
- sea_mask: int32 [128, 512], P('lat', 'lon'), may hold values 0 or 1
- x_taps: float32 [6, 21], P('var'), may hold values from 0.02 to 0.3
- y_taps: float32 [6, 21], P('var'), may hold values from 0.02 to 0.3
- z_taps: float32 [6, 4], P('var'), may hold values from 0.05 to 0.5
- column_weight: float32 [3, 4], replicated, may hold values from 0.1 to 0.5
- balance: float32 [3, 3, 4], replicated, may hold values from -1.5 to 1.5
Outputs:
- increment: float32 [6, 4, 128, 512], P('var', None, 'lat', 'lon')
- control_gradient: float32 [6, 4, 128, 512], P('var', None, 'lat', 'lon')
The draws below stay inside these ranges and needn't reach their ends.
All inputs are finite; a program needn't handle non-finite values. No bound on the sum of `sea_mask` on one device may be relied on, other than what follows from the above.
Results may differ from the reference program's by a relative error of at most 0.00007.
Values sent between devices are 32-bit elements; how exact they have to be, the bound alone decides.
A program may use at most 64 MiB of HBM per device.

```python
import math
import jax
import jax.numpy as jnp
from jax import lax

VARS = 6
RADIUS = 20
NZ = 4
NY = 128
NX = 512


def place_ends(result, rng, least, top_value):
    index_at = [jax.random.randint(jax.random.fold_in(rng, axis), (), 0, length) for axis, length in enumerate(result.shape)]
    main_axis = result.shape.index(max(result.shape))
    next_to = index_at[:main_axis] + [(index_at[main_axis] + 1) % result.shape[main_axis]] + index_at[main_axis + 1:]
    return result.at[tuple(index_at)].set(least).at[tuple(next_to)].set(top_value)


def shard_levels(stream_key, extent, split, smallest, high):
    def one(position, shards_of):
        heights = jax.random.uniform(jax.random.fold_in(jax.random.fold_in(stream_key, 6), position), (shards_of,), jnp.float32, smallest / len(split), high / len(split))
        return jnp.repeat(jnp.exp(heights), extent[position] // shards_of).reshape((-1,) + (1,) * (len(extent) - position - 1))

    level = one(*split[0])
    for cut in split[1:]:
        level = level * one(*cut)
    return level


def normal_values(rng, extent, width, most, split=(), kind=jnp.bfloat16):
    values = width * jax.random.normal(rng, extent, jnp.float32)
    if split:
        values = values * shard_levels(rng, extent, split, -0.22, 0.18)
    return jnp.clip(values, -most, most).astype(kind)


def setup_inputs(seed: int = 0) -> dict:
    key_list = jax.random.split(jax.random.key(seed), 10)
    control = normal_values(key_list[0], (VARS, NZ, NY, NX), 1.0, 6.0, ((0, 2), (2, 4), (3, 4)), jnp.float32)
    gradient = normal_values(key_list[1], (VARS, NZ, NY, NX), 1.0, 6.0, ((0, 2), (2, 4), (3, 4)), jnp.float32)
    std_dev = jnp.clip(jnp.exp(math.log(3.0) - 2.3025851 * jax.random.uniform(key_list[2], (VARS, NY, NX), jnp.float32) ** shard_levels(key_list[2], (VARS, NY, NX), ((0, 2), (1, 4), (2, 4)), -0.2, 0.2)), 0.3, 3.0)
    sea_mask = place_ends((jax.random.randint(key_list[3], (NY, NX), 0, 4) < 3).astype(jnp.int32), jax.random.fold_in(key_list[3], 1), 0, 1)
    x_taps = jnp.clip(jnp.exp(math.log(0.3) - 2.7080503 * jax.random.uniform(key_list[4], (VARS, RADIUS + 1), jnp.float32) ** shard_levels(key_list[4], (VARS, RADIUS + 1), ((0, 2),), -0.2, 0.2)), 0.02, 0.3)
    y_taps = jnp.clip(jnp.exp(math.log(0.3) - 2.7080503 * jax.random.uniform(key_list[5], (VARS, RADIUS + 1), jnp.float32) ** shard_levels(key_list[5], (VARS, RADIUS + 1), ((0, 2),), -0.2, 0.2)), 0.02, 0.3)
    z_taps = jnp.clip(jnp.exp(math.log(0.5) - 2.3025851 * jax.random.uniform(key_list[6], (VARS, NZ), jnp.float32) ** shard_levels(key_list[6], (VARS, NZ), ((0, 2),), -0.2, 0.2)), 0.05, 0.5)
    column_weight = jnp.clip(jnp.exp(jax.random.uniform(key_list[7], (VARS // 2, NZ), jnp.float32, math.log(0.1), math.log(0.5))), 0.1, 0.5)
    balance = normal_values(key_list[8], (VARS // 2, VARS // 2, NZ), 0.3, 1.5, (), jnp.float32)
    return {"control": control, "gradient": gradient, "std_dev": std_dev, "sea_mask": sea_mask, "x_taps": x_taps, "y_taps": y_taps, "z_taps": z_taps, "column_weight": column_weight, "balance": balance}


precise_mode = lax.Precision.HIGHEST


def symmetric_taps(half_taps):
    return jnp.concatenate([half_taps[:, ::-1], half_taps[:, 1:]], axis=1)


def velocity_signs(first_var, count):
    global_var = first_var + jnp.arange(count, dtype=jnp.int32)
    return jnp.where((global_var == 3) | (global_var == 4), jnp.float32(-1.0), jnp.float32(1.0)).astype(jnp.float32)


def filter_x(plane_field, taps_x):
    summed = jnp.zeros(plane_field.shape, jnp.float32)
    for tap_index in range(2 * RADIUS + 1):
        summed = summed + taps_x[tap_index] * jnp.roll(plane_field, RADIUS - tap_index, axis=1)
    return summed


def filter_y(plane_field, taps_y, flip_sign):
    folded = flip_sign * plane_field[NY - RADIUS - 1:NY - 1][::-1, ::-1]
    padded = jnp.concatenate([jnp.zeros((RADIUS, NX), jnp.float32), plane_field, folded], axis=0)
    summed = jnp.zeros(plane_field.shape, jnp.float32)
    for tap_index in range(2 * RADIUS + 1):
        summed = summed + taps_y[tap_index] * padded[tap_index:tap_index + NY]
    return summed


def correlate(values, x_taps, y_taps, z_taps):
    taps_x = symmetric_taps(x_taps)
    taps_y = symmetric_taps(y_taps)
    signs = velocity_signs(0, VARS)
    flattened = values.reshape(VARS * NZ, NY, NX)

    def filter_plane(item):
        plane_field, item_x, item_y, item_sign = item
        return filter_y(filter_x(plane_field, item_x), item_y, item_sign)

    filtered = lax.map(filter_plane, (flattened, jnp.repeat(taps_x, NZ, axis=0), jnp.repeat(taps_y, NZ, axis=0), jnp.repeat(signs, NZ)))
    filtered = filtered.reshape(VARS, NZ, NY, NX)
    level_index = jnp.arange(NZ, dtype=jnp.int32)
    distance = jnp.abs(level_index[:, None] - level_index[None, :])
    zmat = z_taps[:, distance]
    return jnp.einsum('vzw,vwyx->vzyx', zmat, filtered, precision=precise_mode)


def reference(control, gradient, std_dev, sea_mask, x_taps, y_taps, z_taps, column_weight, balance):
    first_half = VARS // 2
    scaled = std_dev * sea_mask.astype(jnp.float32)[None]
    shaped = correlate(control, x_taps, y_taps, z_taps) * scaled[:, None]
    column = jnp.einsum('bz,bzyx->byx', column_weight, shaped[:first_half], precision=precise_mode)
    increment = jnp.concatenate([shaped[:first_half], shaped[first_half:] + jnp.einsum('abz,byx->azyx', balance, column, precision=precise_mode)], axis=0)
    pulled = jnp.einsum('abz,azyx->byx', balance, gradient[first_half:], precision=precise_mode)
    adjusted = jnp.concatenate([gradient[:first_half] + column_weight[:, :, None, None] * pulled[:, None], gradient[first_half:]], axis=0)
    adjusted = adjusted * scaled[:, None]
    control_gradient = correlate(adjusted, x_taps, y_taps, z_taps)
    return (increment, control_gradient)
```

```python
import functools
import jax
import jax.numpy as jnp
from jax import lax
from jax.experimental import pallas as pl
from jax.experimental.pallas import tpu as pltpu
from jax.sharding import PartitionSpec as P

F32 = jnp.float32
BF16 = jnp.bfloat16
MESH = pl.DeviceIdType.MESH


def halves(value):
    high = value.astype(BF16)
    low = (value - high.astype(F32)).astype(BF16)
    return high, low


def dot(left, right):
    return jnp.dot(left, right, preferred_element_type=F32)


def tap_select(distance, taps, var, radius):
    total = jnp.zeros(distance.shape, F32)
    for tap in range(radius + 1):
        total = jnp.where(distance == tap, taps[var, tap], total)
    return total


def kernel(
    sizes,
    control_hbm, gradient_hbm, std_hbm, mask_hbm, xt_hbm, yt_hbm, zt_hbm, cw_hbm, bal_hbm,
    inc_ref, cg_ref,
    xt, yt, zt, cw, bal, con, gra, std, mask, bands_x, bands_y, rows_out, rows_in, lanes_out, lanes_in,
    pad, col_out, col_in,
    relay, fold, load_sem, rows_ss, rows_rs, relay_ss, relay_rs, fold_ss, fold_rs, lanes_ss, lanes_rs, col_ss, col_rs, token,
):
    lats, lons, radius = sizes
    nv, nz, ny, nx = con.shape
    half = nz // 2
    lat, lon, var = lax.axis_index("lat"), lax.axis_index("lon"), lax.axis_index("var")
    top, bottom, upper = lat == lats - 1, lat == 0, var == 1
    east, west = lax.rem(lon + 1, lons), lax.rem(lon + lons - 1, lons)
    mirror = lons - 1 - lon
    other = 1 - var
    relays = lats >= 4 and lats % 2 == 0
    parity = lax.rem(lat, 2)
    step = 2 * parity - 1
    ahead, behind = lat + 2 * step, lat - 2 * step
    turning = (ahead >= 0) & (ahead < lats) & relays
    relaying = (behind >= 0) & (behind < lats) & relays
    far = (mirror != lon) & relays
    folding = far & (lat == lats - 3)
    chunk = nz * radius // 2

    def rdma(src, dst, ss, rs, where):
        return pltpu.make_async_remote_copy(
            src_ref=src, dst_ref=dst, send_sem=ss, recv_sem=rs, device_id=where, device_id_type=MESH
        )

    loads = [
        pltpu.make_async_copy(src, dst, load_sem.at[i])
        for i, (src, dst) in enumerate(
            (
                (control_hbm, con), (gradient_hbm, gra), (std_hbm, std), (mask_hbm, mask),
                (xt_hbm, xt), (yt_hbm, yt), (zt_hbm, zt), (cw_hbm, cw), (bal_hbm, bal),
            )
        )
    ]
    for load in loads:
        load.start()

    barrier = pltpu.get_barrier_semaphore()
    off_top, off_bottom = jnp.logical_not(top), jnp.logical_not(bottom)
    pl.semaphore_signal(barrier, inc=1, device_id={"var": other}, device_id_type=MESH)

    def greet(condition, where):
        @pl.when(condition)
        def _():
            pl.semaphore_signal(barrier, inc=1, device_id=where, device_id_type=MESH)

    greet(off_top, {"lat": lat + 1, "var": 0})
    greet(off_bottom, {"lat": lat - 1, "var": 0})
    greet(turning, {"lat": ahead, "var": 0})
    greet(relaying, {"lat": behind, "var": 0})
    pl.semaphore_signal(barrier, inc=1, device_id={"lon": east, "var": 1}, device_id_type=MESH)
    pl.semaphore_signal(barrier, inc=1, device_id={"lon": west, "var": 1}, device_id_type=MESH)
    greet(top, {"lon": mirror, "var": 1})
    greet(top & far, {"lat": lat - 2, "lon": mirror, "var": 1})
    greet(folding, {"lat": lat + 2, "lon": mirror, "var": 1})
    count = lambda condition: jnp.where(condition, 1, 0)
    greeted_lat = 1 + 2 * (count(off_top) + count(off_bottom) + count(turning) + count(relaying))
    greeted_lon = 5 + 2 * (count(top) + count((top & far) | folding))

    def hear(mine, greeted):
        @pl.when(mine)
        def _():
            pl.semaphore_wait(barrier, greeted)
            pl.semaphore_signal(token, inc=1, device_id={"var": other}, device_id_type=MESH)

        @pl.when(jnp.logical_not(mine))
        def _():
            pl.semaphore_wait(token, 1)

    lane = lax.broadcasted_iota(jnp.int32, (half * ny, nx), 1)
    backwards = nx - 1 - lax.broadcasted_iota(jnp.int32, (ny, nx), 1)

    def part(h):
        return pl.ds(h * chunk, chunk)

    def go(condition, field, way, v, h, dst, rs, where):
        @pl.when(condition)
        def _():
            rdma(rows_out.at[way, field, v, part(h)], dst, rows_ss.at[way], rs, where).start()

    def send_rows(field, v):
        up_rs, down_rs = rows_rs.at[0, field, v], rows_rs.at[1, field, v]
        for h in (1, 0):
            up, down = rows_in.at[0, field, v, part(h)], rows_in.at[1, field, v, part(h)]
            below_top, above_bottom = off_top, off_bottom
            if h == 1 and relays:
                odd = parity == 1
                go(top & far, field, 0, v, h, fold.at[field, v], fold_rs.at[field, v], {"lat": lat - 2})
                go(below_top & odd, field, 0, v, h, relay.at[field, v], relay_rs.at[field, v], {"lat": lat + 2})
                go(above_bottom & jnp.logical_not(odd), field, 1, v, h, relay.at[field, v], relay_rs.at[field, v],
                   {"lat": lat - 2})
                below_top = below_top & jnp.logical_not(odd)
                above_bottom = above_bottom & odd
            go(below_top, field, 0, v, h, up, up_rs, {"lat": lat + 1})
            go(above_bottom, field, 1, v, h, down, down_rs, {"lat": lat - 1})

    def send_mirror(field, v):
        for h in (1, 0):
            go(top & jnp.logical_not(far) if h == 1 else top, field, 0, v, h, rows_in.at[1, field, v, part(h)],
               rows_rs.at[1, field, v], {"lon": mirror})

    def any_rows(field, way, v):
        return rdma(rows_out.at[way, field, v], rows_in.at[way, field, v], rows_ss.at[way], rows_rs.at[way, field, v],
                    {"lon": east})

    def relay_copy(field, v):
        way = 1 - parity
        return rdma(relay.at[field, v], rows_in.at[way, field, v, part(1)], relay_ss.at[0], rows_rs.at[way, field, v],
                    {"lat": lat - step})

    def relay_arrival(field, v):
        return rdma(relay.at[field, v], relay.at[field, v], relay_ss.at[0], relay_rs.at[field, v], {"lon": east})

    def fold_copy(field, v):
        return rdma(fold.at[field, v], rows_in.at[1, field, v, part(1)], fold_ss.at[0], rows_rs.at[1, field, v],
                    {"lat": lat + 2, "lon": mirror})

    def fold_arrival(field, v):
        return rdma(fold.at[field, v], fold.at[field, v], fold_ss.at[0], fold_rs.at[field, v], {"lon": east})

    def pass_rows(field):
        if not relays:
            return
        for v in range(nv):
            @pl.when(relaying)
            def _():
                relay_arrival(field, v).wait_recv()
                relay_copy(field, v).start()

        @pl.when(folding)
        def _():
            for v in range(nv):
                fold_arrival(field, v).wait_recv()
                fold_copy(field, v).start()

    def pack_rows(field, v, planes):
        for z in range(nz):
            rows_out[1, field, v, z * radius:(z + 1) * radius] = planes[z][:radius]

        @pl.when(top)
        def _():
            for z in range(nz):
                turned = jnp.take_along_axis(planes[z], backwards, axis=1)
                rows_out[0, field, v, z * radius:(z + 1) * radius] = turned[ny - radius - 1:ny - 1]

        @pl.when(jnp.logical_not(top))
        def _():
            for z in range(nz):
                rows_out[0, field, v, z * radius:(z + 1) * radius] = planes[z][ny - radius:]

    def pack_lanes(field, flats):
        last = jnp.zeros((half * ny, nx), F32)
        first = jnp.zeros((half * ny, nx), F32)
        for h in range(2):
            for v in range(nv):
                start = (h * nv + v) * radius
                inside = (lane >= start) & (lane < start + radius)
                block = flats[v][h * half * ny:(h + 1) * half * ny]
                last = jnp.where(inside, pltpu.roll(block, (start - (nx - radius)) % nx, 1), last)
                first = jnp.where(inside, pltpu.roll(block, start, 1) if start else block, first)
        lanes_out[field, 0] = last
        lanes_out[field, 1] = first

    def lanes_copy(field, side):
        return rdma(lanes_out.at[field, side], lanes_in.at[field, side], lanes_ss.at[0], lanes_rs.at[field],
                    {"lon": east if side == 0 else west})

    def lanes_arrival(field):
        return rdma(lanes_out.at[field], lanes_in.at[field], lanes_ss.at[0], lanes_rs.at[field], {"lon": east})

    def filter_x(field, v, flat):
        last, first = lanes_in[field, 0], lanes_in[field, 1]
        wraps = []
        for h in range(2):
            start = (h * nv + v) * radius
            from_west = pltpu.roll(last, (nx - radius - start) % nx, 1)
            from_east = pltpu.roll(first, (-start) % nx, 1) if start else first
            wraps.append(jnp.where(lane >= nx - radius, from_west, jnp.where(lane < radius, from_east, 0.0)))
        high, low = halves(jnp.concatenate([flat, jnp.concatenate(wraps, axis=0)], axis=1))
        both = dot(high, bands_x[v])
        return both[:, :nx] + both[:, nx:] + dot(low, bands_x[v, :, :nx])

    span = ny + 2 * radius

    def filter_y(field, v, planes):
        for z in range(nz):
            cols = slice(z * nx, (z + 1) * nx)
            part = slice(z * radius, (z + 1) * radius)
            pad[v, :ny, cols] = planes[z]
            pad[v, ny:ny + radius, cols] = rows_in[0, field, v, part]
            pad[v, ny + radius:span, cols] = rows_in[1, field, v, part]
        high, low = halves(pad[v])
        both = dot(bands_y[v, :, :span], high)
        return both[:ny] + both[ny:] + dot(bands_y[v, :ny, :span], low)

    def filter_z(v, levels):
        out = []
        for z in range(nz):
            total = zt[v, z] * levels[0]
            for w in range(1, nz):
                total = total + zt[v, abs(z - w)] * levels[w]
            out.append(total)
        return out

    @pl.when(bottom)
    def _():
        rows_in[0] = jnp.zeros(rows_in.shape[1:], F32)

    loads[0].wait()
    for v in range(nv):
        pack_rows(0, v, [con[v, z] for z in range(nz)])
    loads[1].wait()
    for load in loads[4:]:
        load.wait()

    @pl.when(upper)
    def _():
        for b in range(nv):
            total = jnp.zeros((ny, nx), F32)
            for a in range(nv):
                for z in range(nz):
                    total = total + bal[a, b, z] * gra[a, z]
            col_out[0, b] = total

    def col_copy(which):
        return rdma(col_out.at[which], col_in.at[which], col_ss.at[0], col_rs.at[0], {"var": other})

    hear(jnp.logical_not(upper), greeted_lat)

    @pl.when(upper)
    def _():
        col_copy(0).start()

    for v in range(nv):
        send_rows(0, v)

    loads[2].wait()
    loads[3].wait()
    sea = mask[...].astype(F32)
    for v in range(nv):
        std[v] = std[v] * sea

    @pl.when(upper)
    def _():
        for v in range(nv):
            for z in range(nz):
                gra[v, z] = gra[v, z] * std[v]

    @pl.when(jnp.logical_not(upper))
    def _():
        col_copy(0).wait_recv()
        for v in range(nv):
            for z in range(nz):
                gra[v, z] = (gra[v, z] + cw[v, z] * col_in[0, v]) * std[v]

    flats = [gra[v].reshape(nz * ny, nx) for v in range(nv)]
    pack_lanes(1, flats)

    circle = lax.broadcasted_iota(jnp.int32, (8, nx), 1)
    circle = jnp.minimum(circle, nx - circle)
    apart = jnp.abs(
        lax.broadcasted_iota(jnp.int32, (nx, nx), 0) - lax.broadcasted_iota(jnp.int32, (nx, nx), 1)
    )
    row = lax.broadcasted_iota(jnp.int32, (ny, nx), 0)
    slot = lax.broadcasted_iota(jnp.int32, (ny, nx), 1)
    below = jnp.where(bottom, 2 * span, row + radius - (slot - ny))
    beyond = slot - (ny + radius)
    above = jnp.where(top, ny - 1 + radius - beyond - row, ny + beyond - row)
    distance = jnp.where(slot < ny, jnp.abs(row - slot), jnp.where(slot < ny + radius, below, above))
    distance = jnp.where(slot < span, distance, 2 * span)
    for v in range(nv):
        ring = tap_select(circle, xt, v, radius)
        full = pltpu.roll(jnp.broadcast_to(ring[:1], (nx, nx)), 0, 1, stride=1, stride_axis=0)
        near = jnp.where(apart <= radius, full, 0.0)
        wrap = jnp.where(apart <= radius, 0.0, full)
        bands_x[v, :nx, :nx], bands_x[v, :nx, nx:] = halves(near)
        bands_x[v, nx:, :nx], bands_x[v, nx:, nx:] = halves(wrap)
        band = tap_select(distance, yt, v, radius)
        number = var * nv + v
        sign = jnp.where(top & ((number == 3) | (number == 4)), -1.0, 1.0).astype(F32)
        band = jnp.where(slot >= ny + radius, band * sign, band)
        bands_y[v, :ny], bands_y[v, ny:] = halves(band)

    hear(upper, greeted_lon)
    for side in range(2):
        lanes_copy(1, side).start()
    for v in range(nv):
        send_mirror(0, v)
    pass_rows(0)
    lanes_arrival(1).wait_recv()
    for v in range(nv):
        flat = filter_x(1, v, gra[v].reshape(nz * ny, nx))
        gra[v] = flat.reshape(nz, ny, nx)
        pack_rows(1, v, [flat[z * ny:(z + 1) * ny] for z in range(nz)])
        send_rows(1, v)
        send_mirror(1, v)

    def wait_rows(field, v):
        any_rows(field, 1, v).wait_recv()

        @pl.when(off_bottom)
        def _():
            any_rows(field, 0, v).wait_recv()

    flats = []
    for v in range(nv):
        wait_rows(0, v)
        out = filter_y(0, v, [con[v, z] for z in range(nz)])
        for z in range(nz):
            con[v, z] = out[:, z * nx:(z + 1) * nx]
    pack_lanes(0, [con[v].reshape(nz * ny, nx) for v in range(nv)])
    for side in range(2):
        lanes_copy(0, side).start()
    pass_rows(1)
    lanes_arrival(0).wait_recv()
    for v in range(nv):
        flat = filter_x(0, v, con[v].reshape(nz * ny, nx))
        levels = filter_z(v, [flat[z * ny:(z + 1) * ny] for z in range(nz)])
        total = jnp.zeros((ny, nx), F32)
        for z in range(nz):
            shaped = levels[z] * std[v]
            con[v, z] = shaped
            inc_ref[v, z] = shaped
            total = total + cw[v, z] * shaped
        col_out[1, v] = total

    @pl.when(jnp.logical_not(upper))
    def _():
        col_copy(1).start()

    for v in range(nv):
        wait_rows(1, v)
        out = filter_y(1, v, [gra[v, z] for z in range(nz)])
        levels = filter_z(v, [out[:, z * nx:(z + 1) * nx] for z in range(nz)])
        for z in range(nz):
            cg_ref[v, z] = levels[z]

    @pl.when(upper)
    def _():
        col_copy(1).wait_recv()
        for a in range(nv):
            for z in range(nz):
                total = con[a, z]
                for b in range(nv):
                    total = total + bal[a, b, z] * col_in[1, b]
                inc_ref[a, z] = total

    def drain(src, dst, sem, condition):
        @pl.when(condition)
        def _():
            rdma(src, dst, sem, sem, {"lon": east}).wait_send()

    col_copy(0).wait_send()
    rdma(lanes_out, lanes_in, lanes_ss.at[0], lanes_rs.at[0], {"lon": east}).wait_send()
    drain(rows_out.at[0], rows_in.at[0], rows_ss.at[0], lat >= 0)
    drain(rows_out.at[1], rows_in.at[1], rows_ss.at[1], off_bottom)
    if relays:
        drain(relay, relay, relay_ss.at[0], relaying)
        drain(fold, fold, fold_ss.at[0], folding)


def store(inc, cg, inc_out, cg_out, sems):
    copies = [pltpu.make_async_copy(src, dst, sems.at[i]) for i, (src, dst) in enumerate(((inc, inc_out), (cg, cg_out)))]
    for copy in copies:
        copy.start()
    for copy in copies:
        copy.wait()


def per_device(lats, lons, control, gradient, std_dev, sea_mask, x_taps, y_taps, z_taps, column_weight, balance):
    nv, nz, ny, nx = control.shape
    radius = x_taps.shape[1] - 1
    span = ny + 2 * radius
    anywhere = pl.BlockSpec(memory_space=pl.ANY)
    vmem = pl.BlockSpec(memory_space=pltpu.VMEM)
    dma = pltpu.SemaphoreType.DMA
    outs = pl.pallas_call(
        functools.partial(kernel, (lats, lons, radius)),
        out_shape=(pltpu.VMEM(control.shape, F32),) * 2,
        in_specs=[anywhere] * 9,
        out_specs=(vmem, vmem),
        scratch_shapes=[pltpu.SMEM(a.shape, F32) for a in (x_taps, y_taps, z_taps, column_weight, balance)] + [
            pltpu.VMEM(control.shape, F32),
            pltpu.VMEM(control.shape, F32),
            pltpu.VMEM(std_dev.shape, F32),
            pltpu.VMEM(sea_mask.shape, jnp.int32),
            pltpu.VMEM((nv, 2 * nx, 2 * nx), BF16),
            pltpu.VMEM((nv, 2 * ny, nx), BF16),
            pltpu.VMEM((2, 2, nv, nz * radius, nx), F32),
            pltpu.VMEM((2, 2, nv, nz * radius, nx), F32),
            pltpu.VMEM((2, 2, nz // 2 * ny, nx), F32),
            pltpu.VMEM((2, 2, nz // 2 * ny, nx), F32),
            pltpu.VMEM((nv, span, nz * nx), F32),
            pltpu.VMEM((2, nv, ny, nx), F32),
            pltpu.VMEM((2, nv, ny, nx), F32),
            pltpu.VMEM((2, nv, nz * radius // 2, nx), F32),
            pltpu.VMEM((2, nv, nz * radius // 2, nx), F32),
            dma((9,)),
            dma((2,)),
            dma((2, 2, nv)),
            dma((1,)),
            dma((2, nv)),
            dma((1,)),
            dma((2, nv)),
            dma((1,)),
            dma((2,)),
            dma((1,)),
            dma((1,)),
            pltpu.SemaphoreType.REGULAR,
        ],
        compiler_params=pltpu.CompilerParams(collective_id=0, has_side_effects=True),
    )(control, gradient, std_dev, sea_mask, x_taps, y_taps, z_taps, column_weight, balance)
    return pl.pallas_call(
        store,
        out_shape=(jax.ShapeDtypeStruct(control.shape, F32),) * 2,
        in_specs=[anywhere] * 2,
        out_specs=(anywhere,) * 2,
        scratch_shapes=[dma((2,))],
        compiler_params=pltpu.CompilerParams(vmem_limit_bytes=1 << 20),
    )(*outs)


def solution(mesh):
    in_specs = (
        P("var", None, "lat", "lon"),
        P("var", None, "lat", "lon"),
        P("var", "lat", "lon"),
        P("lat", "lon"),
        P("var", None),
        P("var", None),
        P("var", None),
        P(),
        P(),
    )
    out_specs = (P("var", None, "lat", "lon"), P("var", None, "lat", "lon"))
    body = functools.partial(per_device, mesh.shape["lat"], mesh.shape["lon"])
    return jax.shard_map(body, mesh=mesh, in_specs=in_specs, out_specs=out_specs, check_vma=False)
```

```python
import functools
import jax
import jax.numpy as jnp
from jax import lax
from jax.experimental import pallas as pl
from jax.experimental.pallas import tpu as pltpu
from jax.sharding import PartitionSpec as P

F32 = jnp.float32
BF16 = jnp.bfloat16
MESH = pl.DeviceIdType.MESH


def halves(value):
    high = value.astype(BF16)
    low = (value - high.astype(F32)).astype(BF16)
    return high, low


def dot(left, right):
    return jnp.dot(left, right, preferred_element_type=F32)


def tap_select(distance, taps, var, radius):
    total = jnp.zeros(distance.shape, F32)
    for tap in range(radius + 1):
        total = jnp.where(distance == tap, taps[var, tap], total)
    return total


def kernel(
    sizes,
    control_hbm, gradient_hbm, std_hbm, mask_hbm, xt_hbm, yt_hbm, zt_hbm, cw_hbm, bal_hbm,
    inc_ref, cg_ref,
    xt, yt, zt, cw, bal, con, gra, std, mask, bands_x, bands_y, rows_out, rows_in, lanes_out, lanes_in, strips_out, strips_in,
    pad, col_out, col_in,
    relay, fold, load_sem, rows_ss, rows_rs, relay_ss, relay_rs, fold_ss, fold_rs, lanes_ss, lanes_rs, col_ss, col_rs, token, mirrored,
):
    lats, lons, radius = sizes
    nv, nz, ny, nx = con.shape
    half = nz // 2
    lat, lon, var = lax.axis_index("lat"), lax.axis_index("lon"), lax.axis_index("var")
    top, bottom, upper = lat == lats - 1, lat == 0, var == 1
    east, west = lax.rem(lon + 1, lons), lax.rem(lon + lons - 1, lons)
    mirror = lons - 1 - lon
    other = 1 - var
    relays = lats >= 4 and lats % 2 == 0
    parity = lax.rem(lat, 2)
    step = 2 * parity - 1
    ahead, behind = lat + 2 * step, lat - 2 * step
    turning = (ahead >= 0) & (ahead < lats) & relays
    relaying = (behind >= 0) & (behind < lats) & relays
    far = (mirror != lon) & relays
    folding = far & (lat == lats - 3)
    chunk = nz * radius // 2

    def rdma(src, dst, ss, rs, where):
        return pltpu.make_async_remote_copy(
            src_ref=src, dst_ref=dst, send_sem=ss, recv_sem=rs, device_id=where, device_id_type=MESH
        )

    loads = [
        pltpu.make_async_copy(src, dst, load_sem.at[i])
        for i, (src, dst) in enumerate(
            (
                (control_hbm, con), (gradient_hbm, gra), (std_hbm, std), (mask_hbm, mask),
                (xt_hbm, xt), (yt_hbm, yt), (zt_hbm, zt), (cw_hbm, cw), (bal_hbm, bal),
            )
        )
    ]
    for load in loads:
        load.start()

    barrier = pltpu.get_barrier_semaphore()
    off_top, off_bottom = jnp.logical_not(top), jnp.logical_not(bottom)
    pl.semaphore_signal(barrier, inc=1, device_id={"var": other}, device_id_type=MESH)

    def greet(condition, where):
        @pl.when(condition)
        def _():
            pl.semaphore_signal(barrier, inc=1, device_id=where, device_id_type=MESH)

    greet(off_top, {"lat": lat + 1, "var": 1})
    greet(off_bottom, {"lat": lat - 1, "var": 1})
    greet(turning, {"lat": ahead, "var": 1})
    greet(relaying, {"lat": behind, "var": 1})
    pl.semaphore_signal(barrier, inc=1, device_id={"lon": east, "var": 0}, device_id_type=MESH)
    pl.semaphore_signal(barrier, inc=1, device_id={"lon": west, "var": 0}, device_id_type=MESH)
    greet(top, {"lon": mirror, "var": 0})
    count = lambda condition: jnp.where(condition, 1, 0)
    greeted_lat = 1 + 2 * (count(off_top) + count(off_bottom) + count(turning) + count(relaying))
    greeted_lon = 5 + 2 * count(top)

    def hear(condition, mine, greeted):
        @pl.when(condition & mine)
        def _():
            pl.semaphore_wait(barrier, greeted)
            pl.semaphore_signal(token, inc=1, device_id={"var": other}, device_id_type=MESH)

        @pl.when(condition & jnp.logical_not(mine))
        def _():
            pl.semaphore_wait(token, 1)

    lane = lax.broadcasted_iota(jnp.int32, (half * ny, nx), 1)
    backwards = nx - 1 - lax.broadcasted_iota(jnp.int32, (ny, nx), 1)

    def part(h):
        return pl.ds(h * chunk, chunk)

    def go(condition, field, way, v, h, dst, rs, where):
        @pl.when(condition)
        def _():
            rdma(rows_out.at[way, field, v, part(h)], dst, rows_ss.at[way], rs, where).start()

    def send_rows(field, v):
        up_rs, down_rs = rows_rs.at[0, field, v], rows_rs.at[1, field, v]
        for h in (1, 0):
            up, down = rows_in.at[0, field, v, part(h)], rows_in.at[1, field, v, part(h)]
            below_top, above_bottom = off_top, off_bottom
            if h == 1 and relays:
                odd = parity == 1
                go(top & far, field, 0, v, h, fold.at[field, v], fold_rs.at[field, v], {"lat": lat - 2})
                go(below_top & odd, field, 0, v, h, relay.at[field, v], relay_rs.at[field, v], {"lat": lat + 2})
                go(above_bottom & jnp.logical_not(odd), field, 1, v, h, relay.at[field, v], relay_rs.at[field, v],
                   {"lat": lat - 2})
                below_top = below_top & jnp.logical_not(odd)
                above_bottom = above_bottom & odd
            go(below_top, field, 0, v, h, up, up_rs, {"lat": lat + 1})
            go(above_bottom, field, 1, v, h, down, down_rs, {"lat": lat - 1})

    def send_mirror(field, v):
        for h in (1, 0):
            go(top & jnp.logical_not(far) if h == 1 else top, field, 0, v, h, rows_in.at[1, field, v, part(h)],
               rows_rs.at[1, field, v], {"lon": mirror})

    def any_rows(field, way, v):
        return rdma(rows_out.at[way, field, v], rows_in.at[way, field, v], rows_ss.at[way], rows_rs.at[way, field, v],
                    {"lon": east})

    def relay_copy(field, v):
        way = 1 - parity
        return rdma(relay.at[field, v], rows_in.at[way, field, v, part(1)], relay_ss.at[0], rows_rs.at[way, field, v],
                    {"lat": lat - step})

    def relay_arrival(field, v):
        return rdma(relay.at[field, v], relay.at[field, v], relay_ss.at[0], relay_rs.at[field, v], {"lon": east})

    def fold_copy(field, v):
        return rdma(fold.at[field, v], rows_in.at[1, field, v, part(1)], fold_ss.at[0], rows_rs.at[1, field, v],
                    {"lat": lat + 2, "lon": mirror})

    def fold_arrival(field, v):
        return rdma(fold.at[field, v], fold.at[field, v], fold_ss.at[0], fold_rs.at[field, v], {"lon": east})

    def pass_rows(field):
        if not relays:
            return
        for v in range(nv):
            @pl.when(relaying)
            def _():
                relay_arrival(field, v).wait_recv()
                relay_copy(field, v).start()

        @pl.when(folding)
        def _():
            if field == 0:
                pl.semaphore_wait(mirrored, 1)
            for v in range(nv):
                fold_arrival(field, v).wait_recv()
                fold_copy(field, v).start()

    def pack_rows(field, v, planes):
        for z in range(nz):
            rows_out[1, field, v, z * radius:(z + 1) * radius] = planes[z][:radius]

        @pl.when(top)
        def _():
            for z in range(nz):
                turned = jnp.take_along_axis(planes[z], backwards, axis=1)
                rows_out[0, field, v, z * radius:(z + 1) * radius] = turned[ny - radius - 1:ny - 1]

        @pl.when(jnp.logical_not(top))
        def _():
            for z in range(nz):
                rows_out[0, field, v, z * radius:(z + 1) * radius] = planes[z][ny - radius:]

    def pack_lanes(flats):
        last = jnp.zeros((half * ny, nx), F32)
        first = jnp.zeros((half * ny, nx), F32)
        for h in range(2):
            for v in range(nv):
                start = (h * nv + v) * radius
                inside = (lane >= start) & (lane < start + radius)
                block = flats[v][h * half * ny:(h + 1) * half * ny]
                last = jnp.where(inside, pltpu.roll(block, (start - (nx - radius)) % nx, 1), last)
                first = jnp.where(inside, pltpu.roll(block, start, 1) if start else block, first)
        lanes_out[0] = last
        lanes_out[1] = first

    def pack_strip(v, planes):
        last = jnp.zeros((ny, nx), F32)
        first = jnp.zeros((ny, nx), F32)
        for z in range(nz):
            start = z * radius
            inside = (lane[:ny] >= start) & (lane[:ny] < start + radius)
            last = jnp.where(inside, pltpu.roll(planes[z], (start - (nx - radius)) % nx, 1), last)
            first = jnp.where(inside, pltpu.roll(planes[z], start, 1) if start else planes[z], first)
        strips_out[v, 0] = last
        strips_out[v, 1] = first

    def lanes_copy(side):
        return rdma(lanes_out.at[side], lanes_in.at[side], lanes_ss.at[0], lanes_rs.at[0],
                    {"lon": east if side == 0 else west})

    def strip_copy(v, side):
        return rdma(strips_out.at[v, side], strips_in.at[v, side], lanes_ss.at[1], lanes_rs.at[1 + v],
                    {"lon": east if side == 0 else west})

    def send_sides(copy):
        @pl.when(2 * lon < lons)
        def _():
            for side in (1, 0):
                copy(side).start()

        @pl.when(2 * lon >= lons)
        def _():
            for side in (0, 1):
                copy(side).start()

    def lanes_arrival():
        return rdma(lanes_out, lanes_in, lanes_ss.at[0], lanes_rs.at[0], {"lon": east})

    def strip_arrival(v):
        return rdma(strips_out.at[v], strips_in.at[v], lanes_ss.at[1], lanes_rs.at[1 + v], {"lon": east})

    def wrapped(rows, last, first, start):
        from_west = pltpu.roll(last, (nx - radius - start) % nx, 1)
        from_east = pltpu.roll(first, (-start) % nx, 1) if start else first
        spot = lane[:rows]
        return jnp.where(spot >= nx - radius, from_west, jnp.where(spot < radius, from_east, 0.0))

    def lanes_wraps(v):
        return [wrapped(half * ny, lanes_in[0], lanes_in[1], (h * nv + v) * radius) for h in range(2)]

    def strip_wraps(v):
        return [wrapped(ny, strips_in[v, 0], strips_in[v, 1], z * radius) for z in range(nz)]

    def filter_x(v, flat, wraps):
        high, low = halves(jnp.concatenate([flat, jnp.concatenate(wraps, axis=0)], axis=1))
        both = dot(high, bands_x[v])
        return both[:, :nx] + both[:, nx:] + dot(low, bands_x[v, :, :nx])

    span = ny + 2 * radius

    def filter_y(field, v, planes):
        for z in range(nz):
            cols = slice(z * nx, (z + 1) * nx)
            part = slice(z * radius, (z + 1) * radius)
            pad[v, :ny, cols] = planes[z]
            pad[v, ny:ny + radius, cols] = rows_in[0, field, v, part]
            pad[v, ny + radius:span, cols] = rows_in[1, field, v, part]
        high, low = halves(pad[v])
        both = dot(bands_y[v, :, :span], high)
        return both[:ny] + both[ny:] + dot(bands_y[v, :ny, :span], low)

    def filter_z(v, levels):
        out = []
        for z in range(nz):
            total = zt[v, z] * levels[0]
            for w in range(1, nz):
                total = total + zt[v, abs(z - w)] * levels[w]
            out.append(total)
        return out

    @pl.when(bottom)
    def _():
        rows_in[0] = jnp.zeros(rows_in.shape[1:], F32)

    loads[0].wait()
    for v in range(nv):
        pack_rows(0, v, [con[v, z] for z in range(nz)])
    loads[1].wait()
    for load in loads[4:]:
        load.wait()

    @pl.when(upper)
    def _():
        for b in range(nv):
            total = jnp.zeros((ny, nx), F32)
            for a in range(nv):
                for z in range(nz):
                    total = total + bal[a, b, z] * gra[a, z]
            col_out[0, b] = total

    def col_copy(which):
        return rdma(col_out.at[which], col_in.at[which], col_ss.at[0], col_rs.at[0], {"var": other})

    hear(lat >= 0, upper, greeted_lat)

    @pl.when(upper)
    def _():
        col_copy(0).start()

    for v in range(nv):
        send_rows(0, v)

    loads[2].wait()
    loads[3].wait()
    sea = mask[...].astype(F32)
    for v in range(nv):
        std[v] = std[v] * sea

    hear((lon > 0) & jnp.logical_not(upper), jnp.logical_not(upper), greeted_lon)

    @pl.when(upper)
    def _():
        for v in range(nv):
            for z in range(nz):
                gra[v, z] = gra[v, z] * std[v]

    @pl.when(jnp.logical_not(upper))
    def _():
        col_copy(0).wait_recv()
        for v in range(nv):
            for z in range(nz):
                gra[v, z] = (gra[v, z] + cw[v, z] * col_in[0, v]) * std[v]

    flats = [gra[v].reshape(nz * ny, nx) for v in range(nv)]
    pack_lanes(flats)

    hear((lon == 0) | upper, jnp.logical_not(upper), greeted_lon)
    send_sides(lanes_copy)

    @pl.when(top & far)
    def _():
        pl.semaphore_signal(mirrored, inc=1, device_id={"lat": lat - 2}, device_id_type=MESH)

    for v in range(nv):
        send_mirror(0, v)

    circle = lax.broadcasted_iota(jnp.int32, (8, nx), 1)
    circle = jnp.minimum(circle, nx - circle)
    apart = jnp.abs(
        lax.broadcasted_iota(jnp.int32, (nx, nx), 0) - lax.broadcasted_iota(jnp.int32, (nx, nx), 1)
    )
    row = lax.broadcasted_iota(jnp.int32, (ny, nx), 0)
    slot = lax.broadcasted_iota(jnp.int32, (ny, nx), 1)
    below = jnp.where(bottom, 2 * span, row + radius - (slot - ny))
    beyond = slot - (ny + radius)
    above = jnp.where(top, ny - 1 + radius - beyond - row, ny + beyond - row)
    distance = jnp.where(slot < ny, jnp.abs(row - slot), jnp.where(slot < ny + radius, below, above))
    distance = jnp.where(slot < span, distance, 2 * span)
    for v in range(nv):
        ring = tap_select(circle, xt, v, radius)
        full = pltpu.roll(jnp.broadcast_to(ring[:1], (nx, nx)), 0, 1, stride=1, stride_axis=0)
        near = jnp.where(apart <= radius, full, 0.0)
        wrap = jnp.where(apart <= radius, 0.0, full)
        bands_x[v, :nx, :nx], bands_x[v, :nx, nx:] = halves(near)
        bands_x[v, nx:, :nx], bands_x[v, nx:, nx:] = halves(wrap)
        band = tap_select(distance, yt, v, radius)
        number = var * nv + v
        sign = jnp.where(top & ((number == 3) | (number == 4)), -1.0, 1.0).astype(F32)
        band = jnp.where(slot >= ny + radius, band * sign, band)
        bands_y[v, :ny], bands_y[v, ny:] = halves(band)

    pass_rows(0)
    lanes_arrival().wait_recv()
    for v in range(nv):
        flat = filter_x(v, gra[v].reshape(nz * ny, nx), lanes_wraps(v))
        gra[v] = flat.reshape(nz, ny, nx)
        pack_rows(1, v, [flat[z * ny:(z + 1) * ny] for z in range(nz)])
        send_rows(1, v)
        send_mirror(1, v)

    def wait_rows(field, v):
        any_rows(field, 1, v).wait_recv()

        @pl.when(off_bottom)
        def _():
            any_rows(field, 0, v).wait_recv()

    for v in range(nv):
        wait_rows(0, v)
        out = filter_y(0, v, [con[v, z] for z in range(nz)])
        planes = [out[:, z * nx:(z + 1) * nx] for z in range(nz)]
        for z in range(nz):
            con[v, z] = planes[z]
        pack_strip(v, planes)
        send_sides(functools.partial(strip_copy, v))
    pass_rows(1)
    for v in range(nv):
        strip_arrival(v).wait_recv()
        flat = filter_x(v, con[v].reshape(nz * ny, nx), strip_wraps(v))
        levels = filter_z(v, [flat[z * ny:(z + 1) * ny] for z in range(nz)])
        total = jnp.zeros((ny, nx), F32)
        for z in range(nz):
            shaped = levels[z] * std[v]
            con[v, z] = shaped
            inc_ref[v, z] = shaped
            total = total + cw[v, z] * shaped
        col_out[1, v] = total

    @pl.when(jnp.logical_not(upper))
    def _():
        col_copy(1).start()

    for v in range(nv):
        wait_rows(1, v)
        out = filter_y(1, v, [gra[v, z] for z in range(nz)])
        levels = filter_z(v, [out[:, z * nx:(z + 1) * nx] for z in range(nz)])
        for z in range(nz):
            cg_ref[v, z] = levels[z]

    @pl.when(upper)
    def _():
        col_copy(1).wait_recv()
        for a in range(nv):
            for z in range(nz):
                total = con[a, z]
                for b in range(nv):
                    total = total + bal[a, b, z] * col_in[1, b]
                inc_ref[a, z] = total

    def drain(src, dst, sem, condition):
        @pl.when(condition)
        def _():
            rdma(src, dst, sem, sem, {"lon": east}).wait_send()

    col_copy(0).wait_send()
    lanes_arrival().wait_send()
    rdma(strips_out, strips_in, lanes_ss.at[1], lanes_rs.at[1], {"lon": east}).wait_send()
    drain(rows_out.at[0], rows_in.at[0], rows_ss.at[0], lat >= 0)
    drain(rows_out.at[1], rows_in.at[1], rows_ss.at[1], off_bottom)
    if relays:
        drain(relay, relay, relay_ss.at[0], relaying)
        drain(fold, fold, fold_ss.at[0], folding)


def store(inc, cg, inc_out, cg_out, sems):
    copies = [pltpu.make_async_copy(src, dst, sems.at[i]) for i, (src, dst) in enumerate(((inc, inc_out), (cg, cg_out)))]
    for copy in copies:
        copy.start()
    for copy in copies:
        copy.wait()


def per_device(lats, lons, control, gradient, std_dev, sea_mask, x_taps, y_taps, z_taps, column_weight, balance):
    nv, nz, ny, nx = control.shape
    radius = x_taps.shape[1] - 1
    span = ny + 2 * radius
    anywhere = pl.BlockSpec(memory_space=pl.ANY)
    vmem = pl.BlockSpec(memory_space=pltpu.VMEM)
    dma = pltpu.SemaphoreType.DMA
    outs = pl.pallas_call(
        functools.partial(kernel, (lats, lons, radius)),
        out_shape=(pltpu.VMEM(control.shape, F32),) * 2,
        in_specs=[anywhere] * 9,
        out_specs=(vmem, vmem),
        scratch_shapes=[pltpu.SMEM(a.shape, F32) for a in (x_taps, y_taps, z_taps, column_weight, balance)] + [
            pltpu.VMEM(control.shape, F32),
            pltpu.VMEM(control.shape, F32),
            pltpu.VMEM(std_dev.shape, F32),
            pltpu.VMEM(sea_mask.shape, jnp.int32),
            pltpu.VMEM((nv, 2 * nx, 2 * nx), BF16),
            pltpu.VMEM((nv, 2 * ny, nx), BF16),
            pltpu.VMEM((2, 2, nv, nz * radius, nx), F32),
            pltpu.VMEM((2, 2, nv, nz * radius, nx), F32),
            pltpu.VMEM((2, nz // 2 * ny, nx), F32),
            pltpu.VMEM((2, nz // 2 * ny, nx), F32),
            pltpu.VMEM((nv, 2, ny, nx), F32),
            pltpu.VMEM((nv, 2, ny, nx), F32),
            pltpu.VMEM((nv, span, nz * nx), F32),
            pltpu.VMEM((2, nv, ny, nx), F32),
            pltpu.VMEM((2, nv, ny, nx), F32),
            pltpu.VMEM((2, nv, nz * radius // 2, nx), F32),
            pltpu.VMEM((2, nv, nz * radius // 2, nx), F32),
            dma((9,)),
            dma((2,)),
            dma((2, 2, nv)),
            dma((1,)),
            dma((2, nv)),
            dma((1,)),
            dma((2, nv)),
            dma((2,)),
            dma((1 + nv,)),
            dma((1,)),
            dma((1,)),
            pltpu.SemaphoreType.REGULAR,
            pltpu.SemaphoreType.REGULAR,
        ],
        compiler_params=pltpu.CompilerParams(collective_id=0, has_side_effects=True),
    )(control, gradient, std_dev, sea_mask, x_taps, y_taps, z_taps, column_weight, balance)
    return pl.pallas_call(
        store,
        out_shape=(jax.ShapeDtypeStruct(control.shape, F32),) * 2,
        in_specs=[anywhere] * 2,
        out_specs=(anywhere,) * 2,
        scratch_shapes=[dma((2,))],
        compiler_params=pltpu.CompilerParams(vmem_limit_bytes=1 << 20),
    )(*outs)


def solution(mesh):
    in_specs = (
        P("var", None, "lat", "lon"),
        P("var", None, "lat", "lon"),
        P("var", "lat", "lon"),
        P("lat", "lon"),
        P("var", None),
        P("var", None),
        P("var", None),
        P(),
        P(),
    )
    out_specs = (P("var", None, "lat", "lon"), P("var", None, "lat", "lon"))
    body = functools.partial(per_device, mesh.shape["lat"], mesh.shape["lon"])
    return jax.shard_map(body, mesh=mesh, in_specs=in_specs, out_specs=out_specs, check_vma=False)
```

```python
import functools
import jax
import jax.numpy as jnp
from jax import lax
from jax.experimental import pallas as pl
from jax.experimental.pallas import tpu as pltpu
from jax.sharding import PartitionSpec as P

F32 = jnp.float32
BF16 = jnp.bfloat16
MESH = pl.DeviceIdType.MESH


def halves(value):
    high = value.astype(BF16)
    low = (value - high.astype(F32)).astype(BF16)
    return high, low


def dot(left, right):
    return jnp.dot(left, right, preferred_element_type=F32)


def tap_select(distance, taps, var, radius):
    total = jnp.zeros(distance.shape, F32)
    for tap in range(radius + 1):
        total = jnp.where(distance == tap, taps[var, tap], total)
    return total


def kernel(
    sizes,
    control_hbm, gradient_hbm, std_hbm, mask_hbm, xt_hbm, yt_hbm, zt_hbm, cw_hbm, bal_hbm,
    inc_ref, cg_ref,
    xt, yt, zt, cw, bal, con, gra, std, mask, bands_x, bands_y, rows_out, rows_in, lanes_out, lanes_in, strips_out, strips_in,
    pad, col_out, col_in,
    relay, fold, fold_inner, load_sem, rows_ss, rows_rs, relay_ss, relay_rs, fold_ss, fold_rs, lanes_ss, lanes_rs, col_ss, col_rs, token, mirrored,
):
    lats, lons, radius = sizes
    nv, nz, ny, nx = con.shape
    half = nz // 2
    lat, lon, var = lax.axis_index("lat"), lax.axis_index("lon"), lax.axis_index("var")
    top, bottom, upper = lat == lats - 1, lat == 0, var == 1
    east, west = lax.rem(lon + 1, lons), lax.rem(lon + lons - 1, lons)
    mirror = lons - 1 - lon
    other = 1 - var
    relays = lats >= 4 and lats % 2 == 0
    parity = lax.rem(lat, 2)
    step = 2 * parity - 1
    ahead, behind = lat + 2 * step, lat - 2 * step
    turning = (ahead >= 0) & (ahead < lats) & relays
    relaying = (behind >= 0) & (behind < lats) & relays
    far = (mirror != lon) & relays
    inner = far & (2 * jnp.abs(lons - 1 - 2 * lon) < lons)
    folding = far & (lat == lats - 3)
    chunk = nz * radius // 2

    def rdma(src, dst, ss, rs, where):
        return pltpu.make_async_remote_copy(
            src_ref=src, dst_ref=dst, send_sem=ss, recv_sem=rs, device_id=where, device_id_type=MESH
        )

    loads = [
        pltpu.make_async_copy(src, dst, load_sem.at[i])
        for i, (src, dst) in enumerate(
            (
                (control_hbm, con), (gradient_hbm, gra), (std_hbm, std), (mask_hbm, mask),
                (xt_hbm, xt), (yt_hbm, yt), (zt_hbm, zt), (cw_hbm, cw), (bal_hbm, bal),
            )
        )
    ]
    for load in loads:
        load.start()

    barrier = pltpu.get_barrier_semaphore()
    off_top, off_bottom = jnp.logical_not(top), jnp.logical_not(bottom)
    pl.semaphore_signal(barrier, inc=1, device_id={"var": other}, device_id_type=MESH)

    def greet(condition, where):
        @pl.when(condition)
        def _():
            pl.semaphore_signal(barrier, inc=1, device_id=where, device_id_type=MESH)

    greet(off_top, {"lat": lat + 1, "var": 1})
    greet(off_bottom, {"lat": lat - 1, "var": 1})
    greet(turning, {"lat": ahead, "var": 1})
    greet(relaying, {"lat": behind, "var": 1})
    pl.semaphore_signal(barrier, inc=1, device_id={"lon": east, "var": 0}, device_id_type=MESH)
    pl.semaphore_signal(barrier, inc=1, device_id={"lon": west, "var": 0}, device_id_type=MESH)
    greet(top, {"lon": mirror, "var": 0})
    count = lambda condition: jnp.where(condition, 1, 0)
    greeted_lat = 1 + 2 * (count(off_top) + count(off_bottom) + count(turning) + count(relaying))
    greeted_lon = 5 + 2 * count(top)

    def hear(condition, mine, greeted):
        @pl.when(condition & mine)
        def _():
            pl.semaphore_wait(barrier, greeted)
            pl.semaphore_signal(token, inc=1, device_id={"var": other}, device_id_type=MESH)

        @pl.when(condition & jnp.logical_not(mine))
        def _():
            pl.semaphore_wait(token, 1)

    lane = lax.broadcasted_iota(jnp.int32, (half * ny, nx), 1)
    backwards = nx - 1 - lax.broadcasted_iota(jnp.int32, (ny, nx), 1)

    def part(h):
        return pl.ds(h * chunk, chunk)

    def go(condition, field, way, v, piece, dst, rs, where):
        @pl.when(condition)
        def _():
            rdma(rows_out.at[way, field, v, piece], dst, rows_ss.at[way], rs, where).start()

    def straight(condition, field, way, v, piece, where):
        go(condition, field, way, v, piece, rows_in.at[way, field, v, piece], rows_rs.at[way, field, v], where)

    odd, even, whole = parity == 1, parity == 0, pl.ds(0, 2 * chunk)

    def send_rows(field, v):
        if relays:
            if field == 0:
                go(top & far, 0, 0, v, part(1), fold.at[v], fold_rs.at[0, v], {"lat": lat - 2})
            else:
                go(top & inner, 1, 0, v, whole, fold_inner.at[v], fold_rs.at[1, v], {"lat": lat - 2})
            go(off_top & odd, field, 0, v, part(1), relay.at[field, v], relay_rs.at[field, v], {"lat": lat + 2})
            go(off_bottom & even, field, 1, v, part(1), relay.at[field, v], relay_rs.at[field, v], {"lat": lat - 2})
        straight(off_top & even if relays else off_top, field, 0, v, whole, {"lat": lat + 1})
        straight(off_bottom & odd if relays else off_bottom, field, 1, v, whole, {"lat": lat - 1})

    def send_across(field, v):
        if relays:
            straight(off_top & odd, field, 0, v, part(0), {"lat": lat + 1})
            straight(off_bottom & even, field, 1, v, part(0), {"lat": lat - 1})

    def send_mirror(field, v):
        def direct(condition, piece):
            go(condition, field, 0, v, piece, rows_in.at[1, field, v, piece], rows_rs.at[1, field, v], {"lon": mirror})

        if field == 0:
            direct(top & jnp.logical_not(far), part(1))
            direct(top, part(0))
        else:
            direct(top & jnp.logical_not(inner), whole)

    def any_rows(field, way, v):
        return rdma(rows_out.at[way, field, v], rows_in.at[way, field, v], rows_ss.at[way], rows_rs.at[way, field, v],
                    {"lon": east})

    def relay_copy(field, v):
        way = 1 - parity
        return rdma(relay.at[field, v], rows_in.at[way, field, v, part(1)], relay_ss.at[0], rows_rs.at[way, field, v],
                    {"lat": lat - step})

    def relay_arrival(field, v):
        return rdma(relay.at[field, v], relay.at[field, v], relay_ss.at[0], relay_rs.at[field, v], {"lon": east})

    def fold_copy(field, v):
        src, piece = (fold.at[v], part(1)) if field == 0 else (fold_inner.at[v], whole)
        return rdma(src, rows_in.at[1, field, v, piece], fold_ss.at[field], rows_rs.at[1, field, v],
                    {"lat": lat + 2, "lon": mirror})

    def fold_arrival(field, v):
        landed = fold.at[v] if field == 0 else fold_inner.at[v]
        return rdma(landed, landed, fold_ss.at[field], fold_rs.at[field, v], {"lon": east})

    def pass_rows(field):
        if not relays:
            return
        for v in range(nv):
            @pl.when(relaying)
            def _():
                relay_arrival(field, v).wait_recv()
                relay_copy(field, v).start()

        @pl.when(folding if field == 0 else folding & inner)
        def _():
            if field == 0:
                pl.semaphore_wait(mirrored, 1)
            for v in range(nv):
                fold_arrival(field, v).wait_recv()
                fold_copy(field, v).start()

    def pack_rows(field, v, planes):
        for z in range(nz):
            rows_out[1, field, v, z * radius:(z + 1) * radius] = planes[z][:radius]

        @pl.when(top)
        def _():
            for z in range(nz):
                turned = jnp.take_along_axis(planes[z], backwards, axis=1)
                rows_out[0, field, v, z * radius:(z + 1) * radius] = turned[ny - radius - 1:ny - 1]

        @pl.when(jnp.logical_not(top))
        def _():
            for z in range(nz):
                rows_out[0, field, v, z * radius:(z + 1) * radius] = planes[z][ny - radius:]

    def pack_lanes(flats):
        last = jnp.zeros((half * ny, nx), F32)
        first = jnp.zeros((half * ny, nx), F32)
        for h in range(2):
            for v in range(nv):
                start = (h * nv + v) * radius
                inside = (lane >= start) & (lane < start + radius)
                block = flats[v][h * half * ny:(h + 1) * half * ny]
                last = jnp.where(inside, pltpu.roll(block, (start - (nx - radius)) % nx, 1), last)
                first = jnp.where(inside, pltpu.roll(block, start, 1) if start else block, first)
        lanes_out[0] = last
        lanes_out[1] = first

    group = nv * nz // 2

    def pack_strip(g, planes):
        last = jnp.zeros((ny, nx), F32)
        first = jnp.zeros((ny, nx), F32)
        for p in range(group):
            start = p * radius
            inside = (lane[:ny] >= start) & (lane[:ny] < start + radius)
            plane = planes[g * group + p]
            last = jnp.where(inside, pltpu.roll(plane, (start - (nx - radius)) % nx, 1), last)
            first = jnp.where(inside, pltpu.roll(plane, start, 1) if start else plane, first)
        strips_out[g, 0] = last
        strips_out[g, 1] = first

    def lanes_copy(side):
        return rdma(lanes_out.at[side], lanes_in.at[side], lanes_ss.at[0], lanes_rs.at[0],
                    {"lon": east if side == 0 else west})

    def strip_copy(g, side):
        return rdma(strips_out.at[g, side], strips_in.at[g, side], lanes_ss.at[1], lanes_rs.at[1 + g],
                    {"lon": east if side == 0 else west})

    def send_sides(copy):
        @pl.when(2 * lon < lons)
        def _():
            for side in (1, 0):
                copy(side).start()

        @pl.when(2 * lon >= lons)
        def _():
            for side in (0, 1):
                copy(side).start()

    def lanes_arrival():
        return rdma(lanes_out, lanes_in, lanes_ss.at[0], lanes_rs.at[0], {"lon": east})

    def strip_arrival(g):
        return rdma(strips_out.at[g], strips_in.at[g], lanes_ss.at[1], lanes_rs.at[1 + g], {"lon": east})

    def wrapped(rows, last, first, start):
        from_west = pltpu.roll(last, (nx - radius - start) % nx, 1)
        from_east = pltpu.roll(first, (-start) % nx, 1) if start else first
        spot = lane[:rows]
        return jnp.where(spot >= nx - radius, from_west, jnp.where(spot < radius, from_east, 0.0))

    def lanes_wraps(v):
        return [wrapped(half * ny, lanes_in[0], lanes_in[1], (h * nv + v) * radius) for h in range(2)]

    def strip_wraps(v):
        spots = [divmod(v * nz + z, group) for z in range(nz)]
        return [wrapped(ny, strips_in[g, 0], strips_in[g, 1], p * radius) for g, p in spots]

    def filter_x(v, flat, wraps):
        high, low = halves(jnp.concatenate([flat, jnp.concatenate(wraps, axis=0)], axis=1))
        both = dot(high, bands_x[v])
        return both[:, :nx] + both[:, nx:] + dot(low, bands_x[v, :, :nx])

    span = ny + 2 * radius

    def filter_y(field, v, planes):
        for z in range(nz):
            cols = slice(z * nx, (z + 1) * nx)
            part = slice(z * radius, (z + 1) * radius)
            pad[v, :ny, cols] = planes[z]
            pad[v, ny:ny + radius, cols] = rows_in[0, field, v, part]
            pad[v, ny + radius:span, cols] = rows_in[1, field, v, part]
        high, low = halves(pad[v])
        both = dot(bands_y[v, :, :span], high)
        return both[:ny] + both[ny:] + dot(bands_y[v, :ny, :span], low)

    def filter_z(v, levels):
        out = []
        for z in range(nz):
            total = zt[v, z] * levels[0]
            for w in range(1, nz):
                total = total + zt[v, abs(z - w)] * levels[w]
            out.append(total)
        return out

    @pl.when(bottom)
    def _():
        rows_in[0] = jnp.zeros(rows_in.shape[1:], F32)

    loads[0].wait()
    for v in range(nv):
        pack_rows(0, v, [con[v, z] for z in range(nz)])
    loads[1].wait()
    for load in loads[4:]:
        load.wait()

    @pl.when(upper)
    def _():
        for b in range(nv):
            total = jnp.zeros((ny, nx), F32)
            for a in range(nv):
                for z in range(nz):
                    total = total + bal[a, b, z] * gra[a, z]
            col_out[0, b] = total

    def col_copy(which):
        return rdma(col_out.at[which], col_in.at[which], col_ss.at[0], col_rs.at[0], {"var": other})

    hear(lat >= 0, upper, greeted_lat)

    @pl.when(upper)
    def _():
        col_copy(0).start()

    for v in range(nv):
        send_rows(0, v)

    loads[2].wait()
    loads[3].wait()
    sea = mask[...].astype(F32)
    for v in range(nv):
        std[v] = std[v] * sea

    hear((lon > 0) & jnp.logical_not(upper), jnp.logical_not(upper), greeted_lon)

    @pl.when(upper)
    def _():
        for v in range(nv):
            for z in range(nz):
                gra[v, z] = gra[v, z] * std[v]

    @pl.when(jnp.logical_not(upper))
    def _():
        col_copy(0).wait_recv()
        for v in range(nv):
            for z in range(nz):
                gra[v, z] = (gra[v, z] + cw[v, z] * col_in[0, v]) * std[v]

    flats = [gra[v].reshape(nz * ny, nx) for v in range(nv)]
    pack_lanes(flats)

    hear((lon == 0) | upper, jnp.logical_not(upper), greeted_lon)
    send_sides(lanes_copy)

    @pl.when(top & far)
    def _():
        pl.semaphore_signal(mirrored, inc=1, device_id={"lat": lat - 2}, device_id_type=MESH)

    for v in range(nv):
        send_across(0, v)
    for v in range(nv):
        send_mirror(0, v)

    circle = lax.broadcasted_iota(jnp.int32, (8, nx), 1)
    circle = jnp.minimum(circle, nx - circle)
    apart = jnp.abs(
        lax.broadcasted_iota(jnp.int32, (nx, nx), 0) - lax.broadcasted_iota(jnp.int32, (nx, nx), 1)
    )
    row = lax.broadcasted_iota(jnp.int32, (ny, nx), 0)
    slot = lax.broadcasted_iota(jnp.int32, (ny, nx), 1)
    below = jnp.where(bottom, 2 * span, row + radius - (slot - ny))
    beyond = slot - (ny + radius)
    above = jnp.where(top, ny - 1 + radius - beyond - row, ny + beyond - row)
    distance = jnp.where(slot < ny, jnp.abs(row - slot), jnp.where(slot < ny + radius, below, above))
    distance = jnp.where(slot < span, distance, 2 * span)
    for v in range(nv):
        ring = tap_select(circle, xt, v, radius)
        full = pltpu.roll(jnp.broadcast_to(ring[:1], (nx, nx)), 0, 1, stride=1, stride_axis=0)
        near = jnp.where(apart <= radius, full, 0.0)
        wrap = jnp.where(apart <= radius, 0.0, full)
        bands_x[v, :nx, :nx], bands_x[v, :nx, nx:] = halves(near)
        bands_x[v, nx:, :nx], bands_x[v, nx:, nx:] = halves(wrap)
        band = tap_select(distance, yt, v, radius)
        number = var * nv + v
        sign = jnp.where(top & ((number == 3) | (number == 4)), -1.0, 1.0).astype(F32)
        band = jnp.where(slot >= ny + radius, band * sign, band)
        bands_y[v, :ny], bands_y[v, ny:] = halves(band)

    pass_rows(0)
    lanes_arrival().wait_recv()
    for v in range(nv):
        flat = filter_x(v, gra[v].reshape(nz * ny, nx), lanes_wraps(v))
        gra[v] = flat.reshape(nz, ny, nx)
        pack_rows(1, v, [flat[z * ny:(z + 1) * ny] for z in range(nz)])
        send_rows(1, v)
        if v == 0:
            send_mirror(1, v)
    for v in range(nv):
        send_across(1, v)

    def wait_rows(field, v):
        any_rows(field, 1, v).wait_recv()

        @pl.when(off_bottom)
        def _():
            any_rows(field, 0, v).wait_recv()

    planes = []
    for v in range(nv):
        wait_rows(0, v)
        out = filter_y(0, v, [con[v, z] for z in range(nz)])
        for z in range(nz):
            con[v, z] = out[:, z * nx:(z + 1) * nx]
            planes.append(con[v, z])
            if len(planes) % group == 0:
                pack_strip(len(planes) // group - 1, planes)
                send_sides(functools.partial(strip_copy, len(planes) // group - 1))
    for v in range(1, nv):
        send_mirror(1, v)
    pass_rows(1)
    heard = 0
    for v in range(nv):
        while heard * group < (v + 1) * nz:
            strip_arrival(heard).wait_recv()
            heard += 1
        flat = filter_x(v, con[v].reshape(nz * ny, nx), strip_wraps(v))
        levels = filter_z(v, [flat[z * ny:(z + 1) * ny] for z in range(nz)])
        total = jnp.zeros((ny, nx), F32)
        for z in range(nz):
            shaped = levels[z] * std[v]
            con[v, z] = shaped
            inc_ref[v, z] = shaped
            total = total + cw[v, z] * shaped
        col_out[1, v] = total

    @pl.when(jnp.logical_not(upper))
    def _():
        col_copy(1).start()

    for v in range(nv):
        wait_rows(1, v)
        out = filter_y(1, v, [gra[v, z] for z in range(nz)])
        levels = filter_z(v, [out[:, z * nx:(z + 1) * nx] for z in range(nz)])
        for z in range(nz):
            cg_ref[v, z] = levels[z]

    @pl.when(upper)
    def _():
        col_copy(1).wait_recv()
        for a in range(nv):
            for z in range(nz):
                total = con[a, z]
                for b in range(nv):
                    total = total + bal[a, b, z] * col_in[1, b]
                inc_ref[a, z] = total

    def drain(src, dst, sem, condition):
        @pl.when(condition)
        def _():
            rdma(src, dst, sem, sem, {"lon": east}).wait_send()

    col_copy(0).wait_send()
    lanes_arrival().wait_send()
    rdma(strips_out, strips_in, lanes_ss.at[1], lanes_rs.at[1], {"lon": east}).wait_send()
    drain(rows_out.at[0], rows_in.at[0], rows_ss.at[0], lat >= 0)
    drain(rows_out.at[1], rows_in.at[1], rows_ss.at[1], off_bottom)
    if relays:
        drain(relay, relay, relay_ss.at[0], relaying)
        drain(fold, fold, fold_ss.at[0], folding)
        drain(fold_inner, fold_inner, fold_ss.at[1], folding & inner)


def store(inc, cg, inc_out, cg_out, sems):
    copies = [pltpu.make_async_copy(src, dst, sems.at[i]) for i, (src, dst) in enumerate(((inc, inc_out), (cg, cg_out)))]
    for copy in copies:
        copy.start()
    for copy in copies:
        copy.wait()


def per_device(lats, lons, control, gradient, std_dev, sea_mask, x_taps, y_taps, z_taps, column_weight, balance):
    nv, nz, ny, nx = control.shape
    radius = x_taps.shape[1] - 1
    span = ny + 2 * radius
    anywhere = pl.BlockSpec(memory_space=pl.ANY)
    vmem = pl.BlockSpec(memory_space=pltpu.VMEM)
    dma = pltpu.SemaphoreType.DMA
    outs = pl.pallas_call(
        functools.partial(kernel, (lats, lons, radius)),
        out_shape=(pltpu.VMEM(control.shape, F32),) * 2,
        in_specs=[anywhere] * 9,
        out_specs=(vmem, vmem),
        scratch_shapes=[pltpu.SMEM(a.shape, F32) for a in (x_taps, y_taps, z_taps, column_weight, balance)] + [
            pltpu.VMEM(control.shape, F32),
            pltpu.VMEM(control.shape, F32),
            pltpu.VMEM(std_dev.shape, F32),
            pltpu.VMEM(sea_mask.shape, jnp.int32),
            pltpu.VMEM((nv, 2 * nx, 2 * nx), BF16),
            pltpu.VMEM((nv, 2 * ny, nx), BF16),
            pltpu.VMEM((2, 2, nv, nz * radius, nx), F32),
            pltpu.VMEM((2, 2, nv, nz * radius, nx), F32),
            pltpu.VMEM((2, nz // 2 * ny, nx), F32),
            pltpu.VMEM((2, nz // 2 * ny, nx), F32),
            pltpu.VMEM((2, 2, ny, nx), F32),
            pltpu.VMEM((2, 2, ny, nx), F32),
            pltpu.VMEM((nv, span, nz * nx), F32),
            pltpu.VMEM((2, nv, ny, nx), F32),
            pltpu.VMEM((2, nv, ny, nx), F32),
            pltpu.VMEM((2, nv, nz * radius // 2, nx), F32),
            pltpu.VMEM((nv, nz * radius // 2, nx), F32),
            pltpu.VMEM((nv, nz * radius, nx), F32),
            dma((9,)),
            dma((2,)),
            dma((2, 2, nv)),
            dma((1,)),
            dma((2, nv)),
            dma((2,)),
            dma((2, nv)),
            dma((2,)),
            dma((3,)),
            dma((1,)),
            dma((1,)),
            pltpu.SemaphoreType.REGULAR,
            pltpu.SemaphoreType.REGULAR,
        ],
        compiler_params=pltpu.CompilerParams(collective_id=0, has_side_effects=True),
    )(control, gradient, std_dev, sea_mask, x_taps, y_taps, z_taps, column_weight, balance)
    return pl.pallas_call(
        store,
        out_shape=(jax.ShapeDtypeStruct(control.shape, F32),) * 2,
        in_specs=[anywhere] * 2,
        out_specs=(anywhere,) * 2,
        scratch_shapes=[dma((2,))],
        compiler_params=pltpu.CompilerParams(vmem_limit_bytes=1 << 20),
    )(*outs)


def solution(mesh):
    in_specs = (
        P("var", None, "lat", "lon"),
        P("var", None, "lat", "lon"),
        P("var", "lat", "lon"),
        P("lat", "lon"),
        P("var", None),
        P("var", None),
        P("var", None),
        P(),
        P(),
    )
    out_specs = (P("var", None, "lat", "lon"), P("var", None, "lat", "lon"))
    body = functools.partial(per_device, mesh.shape["lat"], mesh.shape["lon"])
    return jax.shard_map(body, mesh=mesh, in_specs=in_specs, out_specs=out_specs, check_vma=False)
```
